32 devices in a mesh: lat: 8 (over z, y), lon: 4 (over x, core).
Axes of the slice: x: 2, y: 2, z: 4, core: 2. Of those that a mesh axis runs over, the one named last changes fastest.
Arguments:
- state_fields: float32 [5, 32, 64, 4096], P(None, None, 'lat', 'lon'), may hold values from -6 to 6
- stencil_weights: float32 [4, 32, 64, 4096], P(None, None, 'lat', 'lon'), may hold values from 0.02 to 0.22
- filter_mask: int32 [64], replicated, may hold values from 0 to 1, as said below
- cutoff_wave: int32 [64], replicated, may hold values from 0 to 255, as said below
Outputs:
- advanced: float32 [5, 32, 64, 4096], P(None, None, 'lat', 'lon')
The draws below stay inside these ranges and needn't reach their ends.
Inputs may be any that keep to these rules, and one draw needn't show every extreme that they name: `filter_mask`: every row outside the first and last 8 rows holds 0. `cutoff_wave`: from 1 to 255 in the first and last 8 rows, 0 elsewhere.
All inputs are finite; a program needn't handle non-finite values.
Results may differ from the reference program's by a relative error of at most 0.0011.
Values may be sent and summed in bfloat16 or wider, within the bound.
A program may use at most 64 MiB of HBM per device.

```python
import math
import jax
import jax.numpy as jnp
from jax import lax

NLON = 4096
FIELDS = 5
LEV = 32
KC = 256
NLAT = 64
POLAR = 8


def polar_row(choice_value):
    return jnp.where(choice_value < POLAR, choice_value, NLAT - 2 * POLAR + choice_value)


def draw_filter_mask(key, part):
    row_ids = jnp.arange(NLAT, dtype=jnp.int32)
    inside = (row_ids < POLAR) | (row_ids >= NLAT - POLAR)
    coins = jax.random.randint(jax.random.fold_in(key, 11), (NLAT,), 0, 4)
    picked = polar_row(jax.random.randint(jax.random.fold_in(key, 12), (), 0, 2 * POLAR))
    chosen = inside & ((coins != 0) | (row_ids == picked))
    return jnp.where(chosen, 1, 0).astype(jnp.int32)


def draw_cutoff_wave(key, part):
    row_ids = jnp.arange(NLAT, dtype=jnp.int32)
    inside = (row_ids < POLAR) | (row_ids >= NLAT - POLAR)
    values = jax.random.randint(jax.random.fold_in(key, 21), (NLAT,), 1, KC)
    lowest = polar_row(jax.random.randint(jax.random.fold_in(key, 22), (), 0, 2 * POLAR))
    highest = polar_row(jax.random.randint(jax.random.fold_in(key, 23), (), 0, 2 * POLAR))
    values = jnp.where(row_ids == lowest, 1, values)
    values = jnp.where(row_ids == highest, KC - 1, values)
    return jnp.where(inside, values, 0).astype(jnp.int32)


def shard_levels(stream_key, extent, split, smallest, high):
    factor_of, own = 1.0, jax.random.fold_in(stream_key, 6)
    for position, shards_of in split:
        heights = jnp.exp(jax.random.uniform(jax.random.fold_in(own, position), (shards_of,), jnp.float32, smallest / len(split), high / len(split)))
        factor_of = factor_of * jnp.repeat(heights, extent[position] // shards_of).reshape([-1 if axis == position else 1 for axis in range(len(extent))])
    return factor_of


def normal_values(rng, extent, deviation, bound, pieces=(), kind=jnp.bfloat16):
    result = jax.random.normal(rng, extent, jnp.float32) * deviation
    if len(pieces) > 0:
        result = shard_levels(rng, extent, pieces, -0.22, 0.18) * result
    return jnp.clip(result, min=-bound, max=bound).astype(kind)


def setup_inputs(seed: int = 0) -> dict:
    streams_of = jax.random.split(jax.random.key(seed), 5)
    state_fields = normal_values(streams_of[0], (FIELDS, LEV, NLAT, NLON), 1.0, 6.0, ((2, 8), (3, 4)), jnp.float32)
    stencil_weights = jnp.clip(0.02 + 0.2 * jax.random.uniform(streams_of[1], (4, LEV, NLAT, NLON), jnp.float32) ** shard_levels(streams_of[1], (4, LEV, NLAT, NLON), ((2, 8), (3, 4)), -0.2, 0.2), 0.02, 0.22)
    filter_mask = draw_filter_mask(jax.random.fold_in(streams_of[4], 71), 0)
    cutoff_wave = draw_cutoff_wave(jax.random.fold_in(streams_of[4], 71), 0)
    return {"state_fields": state_fields, "stencil_weights": stencil_weights, "filter_mask": filter_mask, "cutoff_wave": cutoff_wave}


def wave_table(columns, mode_count, circle_size):
    wavenums = jnp.arange(2 * mode_count, dtype=jnp.int32) % mode_count
    product = (columns[:, None] * wavenums[None, :]) % circle_size
    angles = product.astype(jnp.float32) * (2.0 * math.pi / circle_size)
    upper = jnp.arange(2 * mode_count, dtype=jnp.int32) < mode_count
    return jnp.where(upper[None, :], jnp.cos(angles), jnp.sin(angles)).astype(jnp.bfloat16)


def mode_scale(cutoffs, mode_count, circle_size):
    wavenums = jnp.arange(2 * mode_count, dtype=jnp.int32) % mode_count
    weights = jnp.where(wavenums == 0, 1.0 / circle_size, 2.0 / circle_size).astype(jnp.float32)
    return jnp.where(wavenums[None, :] <= cutoffs[:, None], weights[None, :], jnp.float32(0.0)).astype(jnp.float32)


def reference(state_fields, stencil_weights, filter_mask, cutoff_wave):
    field = state_fields
    wind_signs = jnp.where(jnp.arange(FIELDS) < 2, -1.0, 1.0).astype(jnp.float32)[:, None, None, None]
    turned = jnp.roll(field, NLON // 2, axis=3)
    north_side = jnp.concatenate([wind_signs * turned[:, :, 0:1], field[:, :, :-1]], axis=2)
    south_side = jnp.concatenate([field[:, :, 1:], wind_signs * turned[:, :, -1:]], axis=2)
    east_side = jnp.roll(field, -1, axis=3)
    west_side = jnp.roll(field, 1, axis=3)
    weights = stencil_weights
    stepped = field + weights[0] * (east_side - field) + weights[1] * (west_side - field) + weights[2] * (north_side - field) + weights[3] * (south_side - field)
    band_index = jnp.concatenate([jnp.arange(POLAR, dtype=jnp.int32), jnp.arange(NLAT - POLAR, NLAT, dtype=jnp.int32)]).astype(jnp.int32)
    band_values = stepped[:, :, band_index, :]
    rounded = lax.optimization_barrier(band_values.astype(jnp.bfloat16)).astype(jnp.float32)
    circle_table = lax.optimization_barrier(wave_table(jnp.arange(NLON, dtype=jnp.int32), KC, NLON)).astype(jnp.float32)
    spectra = jnp.dot(rounded.reshape(-1, NLON), circle_table, precision=lax.Precision.HIGHEST)
    spectra = spectra.reshape(FIELDS * LEV, 2 * POLAR, 2 * KC) * mode_scale(cutoff_wave[band_index], KC, NLON)[None]
    spectra = lax.optimization_barrier(spectra.astype(jnp.bfloat16)).astype(jnp.float32)
    smooth = jnp.dot(spectra.reshape(-1, 2 * KC), circle_table.T, precision=lax.Precision.HIGHEST)
    smooth = lax.optimization_barrier(smooth.astype(jnp.bfloat16)).astype(jnp.float32)
    smooth = smooth.reshape(FIELDS, LEV, 2 * POLAR, NLON)
    keep_rows = filter_mask[band_index] == 1
    chosen = jnp.where(keep_rows[None, None, :, None], smooth, band_values)
    return stepped.at[:, :, band_index, :].set(chosen)
```

```python
import math

import jax
import jax.numpy as jnp
from jax import lax
from jax.sharding import PartitionSpec as P

KC = 256


def flip(block, axis, bit):
    count = lax.axis_size(axis)
    route = [(i, i ^ (1 << bit)) for i in range(count) if i ^ (1 << bit) < count]
    return lax.ppermute(block, axis, route)


def shift(block, axis, step, closed):
    count = lax.axis_size(axis)
    route = [(i, (i + step) % count) for i in range(count) if closed or 0 <= i + step < count]
    return lax.ppermute(block, axis, route)


def angle_parts(columns, circle_size):
    waves = jnp.arange(KC, dtype=jnp.int32)
    product = columns[:, None] * waves[None, :] % circle_size
    angles = product.astype(jnp.float32) * (2.0 * math.pi / circle_size)
    return jnp.cos(angles), jnp.sin(angles)


def wave_table(first, column_count, circle_size):
    fine = 32
    coarse = column_count // fine
    cos_c, sin_c = angle_parts(first + fine * jnp.arange(coarse, dtype=jnp.int32), circle_size)
    cos_f, sin_f = angle_parts(jnp.arange(fine, dtype=jnp.int32), circle_size)
    cos_c, sin_c = cos_c[:, None], sin_c[:, None]
    cos_f, sin_f = cos_f[None], sin_f[None]
    table = jnp.concatenate(
        [cos_c * cos_f - sin_c * sin_f, sin_c * cos_f + cos_c * sin_f], axis=2
    )
    return table.astype(jnp.bfloat16).reshape(column_count, 2 * KC)


def mode_scale(cutoffs, circle_size):
    waves = jnp.arange(2 * KC, dtype=jnp.int32) % KC
    weights = jnp.where(waves == 0, 1.0 / circle_size, 2.0 / circle_size).astype(jnp.float32)
    return jnp.where(waves[None, :] <= cutoffs[:, None], weights[None, :], jnp.float32(0.0))


def on_device(state_fields, stencil_weights, filter_mask, cutoff_wave):
    fields, levels, rows, columns = state_fields.shape
    lat_count, lon_count = lax.axis_size("lat"), lax.axis_size("lon")
    lat_pos, lon_pos = lax.axis_index("lat"), lax.axis_index("lon")
    circle_size = columns * lon_count
    bits = lon_count.bit_length() - 1
    first_row = state_fields[:, :, 0]
    last_row = state_fields[:, :, -1]
    signs = jnp.where(jnp.arange(fields) < 2, -1.0, 1.0).astype(jnp.float32)[:, None, None]
    pole_row = jnp.where(lat_pos == 0, first_row, last_row).astype(jnp.bfloat16)
    over_pole = signs * flip(pole_row, "lon", bits - 1).astype(jnp.float32)
    north_in = shift(last_row.astype(jnp.bfloat16), "lat", 1, False).astype(jnp.float32)
    south_in = shift(first_row.astype(jnp.bfloat16), "lat", -1, False).astype(jnp.float32)
    north_edge = jnp.where(lat_pos == 0, over_pole, north_in)
    south_edge = jnp.where(lat_pos == lat_count - 1, over_pole, south_in)
    west_in = shift(state_fields[..., -1], "lon", 1, True)
    east_in = shift(state_fields[..., 0], "lon", -1, True)
    north_side = jnp.concatenate([north_edge[:, :, None], state_fields[:, :, :-1]], axis=2)
    south_side = jnp.concatenate([state_fields[:, :, 1:], south_edge[:, :, None]], axis=2)
    west_side = jnp.concatenate([west_in[..., None], state_fields[..., :-1]], axis=3)
    east_side = jnp.concatenate([state_fields[..., 1:], east_in[..., None]], axis=3)
    stepped = (
        state_fields
        + stencil_weights[0] * (east_side - state_fields)
        + stencil_weights[1] * (west_side - state_fields)
        + stencil_weights[2] * (north_side - state_fields)
        + stencil_weights[3] * (south_side - state_fields)
    )
    items = fields * levels
    start = lat_pos * rows
    cuts = lax.dynamic_slice_in_dim(cutoff_wave, start, rows)
    mask = lax.dynamic_slice_in_dim(filter_mask, start, rows)
    table = wave_table(lon_pos * columns, columns, circle_size)
    rounded = stepped.astype(jnp.bfloat16).reshape(items * rows, columns)
    partial = jnp.dot(rounded, table, preferred_element_type=jnp.float32)
    halves = partial.reshape(2, items * rows // 2, 2 * KC)
    low = lon_pos % 2 == 0
    mine = jnp.where(low, halves[0], halves[1])
    total = mine + flip(jnp.where(low, halves[1], halves[0]), "lon", 0)
    for bit in range(1, bits):
        total = total + flip(total.astype(jnp.float16), "lon", bit).astype(jnp.float32)
    scale = mode_scale(cuts, circle_size)
    spectra = (total.reshape(-1, rows, 2 * KC) * scale[None]).astype(jnp.bfloat16)
    other = flip(spectra, "lon", 0)
    spectra = jnp.concatenate(
        [jnp.where(low, spectra, other), jnp.where(low, other, spectra)], axis=0
    ).reshape(-1, 2 * KC)
    smooth = lax.dot_general(
        spectra, table, (((1,), (1,)), ((), ())), preferred_element_type=jnp.float32
    )
    smooth = smooth.astype(jnp.bfloat16).reshape(fields, levels, rows, columns)
    return jnp.where(mask[None, None, :, None] == 1, smooth.astype(jnp.float32), stepped)


def solution(mesh):
    return jax.shard_map(
        on_device,
        mesh=mesh,
        in_specs=(P(None, None, "lat", "lon"), P(None, None, "lat", "lon"), P(), P()),
        out_specs=P(None, None, "lat", "lon"),
        check_vma=False,
    )
```

```python
import math

import jax
import jax.numpy as jnp
from jax import lax
from jax.experimental import pallas as pl
from jax.experimental.pallas import tpu as pltpu
from jax.sharding import PartitionSpec as P

KC = 256


def flip(block, axis, bit):
    count = lax.axis_size(axis)
    route = [(i, i ^ (1 << bit)) for i in range(count) if i ^ (1 << bit) < count]
    return lax.ppermute(block, axis, route)


def shift(block, axis, step, closed):
    count = lax.axis_size(axis)
    route = [(i, (i + step) % count) for i in range(count) if closed or 0 <= i + step < count]
    return lax.ppermute(block, axis, route)


def angle_parts(columns, circle_size):
    waves = jnp.arange(KC, dtype=jnp.int32)
    product = columns[:, None] * waves[None, :] % circle_size
    angles = product.astype(jnp.float32) * (2.0 * math.pi / circle_size)
    return jnp.cos(angles), jnp.sin(angles)


def wave_table(first, column_count, circle_size):
    fine = 32
    coarse = column_count // fine
    cos_c, sin_c = angle_parts(first + fine * jnp.arange(coarse, dtype=jnp.int32), circle_size)
    cos_f, sin_f = angle_parts(jnp.arange(fine, dtype=jnp.int32), circle_size)
    cos_c, sin_c = cos_c[:, None], sin_c[:, None]
    cos_f, sin_f = cos_f[None], sin_f[None]
    table = jnp.concatenate(
        [cos_c * cos_f - sin_c * sin_f, sin_c * cos_f + cos_c * sin_f], axis=2
    )
    return table.astype(jnp.bfloat16).reshape(column_count, 2 * KC)


def mode_scale(cutoffs, circle_size):
    waves = jnp.arange(2 * KC, dtype=jnp.int32) % KC
    weights = jnp.where(waves == 0, 1.0 / circle_size, 2.0 / circle_size).astype(jnp.float32)
    return jnp.where(waves[None, :] <= cutoffs[:, None], weights[None, :], jnp.float32(0.0))


def step_kernel(
    state, weights, north, south, west, east, table, stepped, partial, rounded
):
    fields, levels, rows, columns = state.shape
    lane = lax.broadcasted_iota(jnp.int32, (rows, columns), 1)
    line = lax.broadcasted_iota(jnp.int32, (rows, columns), 0)

    def one_field(field, carry):
        above = north[field].astype(jnp.float32)
        below = south[field].astype(jnp.float32)
        left = west[0, field]
        right = east[0, field]
        for level in range(0, levels, 2):
            pair = []
            for at in (level, level + 1):
                x = state[field, at]
                w = jnp.where(lane == 0, left[:, at : at + 1], pltpu.roll(x, 1, 1))
                e = jnp.where(
                    lane == columns - 1, right[:, at : at + 1], pltpu.roll(x, columns - 1, 1)
                )
                n = jnp.where(line == 0, above[at : at + 1], pltpu.roll(x, 1, 0))
                s = jnp.where(line == rows - 1, below[at : at + 1], pltpu.roll(x, rows - 1, 0))
                y = (
                    x
                    + weights[0, at] * (e - x)
                    + weights[1, at] * (w - x)
                    + weights[2, at] * (n - x)
                    + weights[3, at] * (s - x)
                )
                stepped[field, at] = y
                pair.append(y)
            first = pl.multiple_of(field * (levels * rows) + level * rows, 2 * rows)
            rounded[pl.ds(first, 2 * rows), :] = jnp.concatenate(pair, axis=0).astype(
                jnp.bfloat16
            )
        return carry

    lax.fori_loop(0, fields, one_field, 0)
    partial[0] = jnp.dot(rounded[...], table[...], preferred_element_type=jnp.float32)


def merge_kernel(keep, spectra, table, stepped, merged):
    fields, levels, rows, columns = stepped.shape
    for field in range(fields):
        first = field * levels * rows
        smooth = lax.dot_general(
            spectra[0, first : first + levels * rows],
            table[...],
            (((1,), (1,)), ((), ())),
            preferred_element_type=jnp.float32,
        )
        smooth = smooth.astype(jnp.bfloat16).astype(jnp.float32)
        smooth = smooth.reshape(levels, rows, columns)
        kept = jnp.broadcast_to(keep[...], (rows, columns))[None] != 0
        merged[field] = jnp.where(kept, smooth, stepped[field])


def chunk_of(fields, levels, rows, columns, size):
    return pl.BlockSpec((fields, size, rows, columns), lambda i: (0, i, 0, 0))


def whole(*shape):
    return pl.BlockSpec(shape, lambda i: (0,) * len(shape), pipeline_mode=pl.Buffered(1))


def on_device(state_fields, stencil_weights, filter_mask, cutoff_wave):
    fields, levels, rows, columns = state_fields.shape
    lat_count, lon_count = lax.axis_size("lat"), lax.axis_size("lon")
    lat_pos, lon_pos = lax.axis_index("lat"), lax.axis_index("lon")
    circle_size = columns * lon_count
    bits = lon_count.bit_length() - 1
    first_row = state_fields[:, :, 0]
    last_row = state_fields[:, :, -1]
    signs = jnp.where(jnp.arange(fields) < 2, -1.0, 1.0).astype(jnp.bfloat16)[:, None, None]
    pole_row = jnp.where(lat_pos == 0, first_row, last_row).astype(jnp.bfloat16)
    over_pole = flip(signs * pole_row, "lon", bits - 1)
    north_in = shift(last_row.astype(jnp.bfloat16), "lat", 1, False)
    south_in = shift(first_row.astype(jnp.bfloat16), "lat", -1, False)
    north_edge = jnp.where(lat_pos == 0, over_pole, north_in)
    south_edge = jnp.where(lat_pos == lat_count - 1, over_pole, south_in)
    size = 8
    steps = levels // size

    def columns_of(edge):
        return edge.reshape(fields, steps, size, rows).transpose(1, 0, 3, 2)

    west_in = shift(columns_of(state_fields[..., -1]), "lon", 1, True)
    east_in = shift(columns_of(state_fields[..., 0]), "lon", -1, True)
    items = fields * levels
    start = lat_pos * rows
    cuts = lax.dynamic_slice_in_dim(cutoff_wave, start, rows)
    mask = lax.dynamic_slice_in_dim(filter_mask, start, rows)
    table = wave_table(lon_pos * columns, columns, circle_size)
    rows_each = fields * size * rows
    halo = pl.BlockSpec((fields, size, columns), lambda i: (0, i, 0))
    side = pl.BlockSpec((1, fields, rows, size), lambda i: (i, 0, 0, 0))
    stepped, partial = pl.pallas_call(
        step_kernel,
        grid=(steps,),
        in_specs=[
            chunk_of(fields, levels, rows, columns, size),
            chunk_of(4, levels, rows, columns, size),
            halo,
            halo,
            side,
            side,
            whole(columns, 2 * KC),
        ],
        out_specs=[
            chunk_of(fields, levels, rows, columns, size),
            pl.BlockSpec((1, rows_each, 2 * KC), lambda i: (i, 0, 0)),
        ],
        out_shape=[
            jax.ShapeDtypeStruct(state_fields.shape, jnp.float32),
            jax.ShapeDtypeStruct((steps, rows_each, 2 * KC), jnp.float32),
        ],
        scratch_shapes=[pltpu.VMEM((rows_each, columns), jnp.bfloat16)],
        name="step",
    )(state_fields, stencil_weights, north_edge, south_edge, west_in, east_in, table)
    halves = partial.reshape(2, items * rows // 2, 2 * KC)
    low = lon_pos % 2 == 0
    mine = jnp.where(low, halves[0], halves[1])
    total = mine + flip(jnp.where(low, halves[1], halves[0]), "lon", 0)
    for bit in range(1, bits):
        total = total + flip(total.astype(jnp.float16), "lon", bit).astype(jnp.float32)
    scale = mode_scale(cuts, circle_size)
    spectra = (total.reshape(-1, rows, 2 * KC) * scale[None]).astype(jnp.bfloat16)
    other = flip(spectra, "lon", 0)
    spectra = jnp.concatenate(
        [jnp.where(low, spectra, other), jnp.where(low, other, spectra)], axis=0
    ).reshape(steps, rows_each, 2 * KC)
    return pl.pallas_call(
        merge_kernel,
        grid=(steps,),
        in_specs=[
            whole(rows, 1),
            pl.BlockSpec((1, rows_each, 2 * KC), lambda i: (i, 0, 0)),
            whole(columns, 2 * KC),
            chunk_of(fields, levels, rows, columns, size),
        ],
        out_specs=chunk_of(fields, levels, rows, columns, size),
        out_shape=jax.ShapeDtypeStruct(state_fields.shape, jnp.float32),
        name="merge",
    )(mask[:, None], spectra, table, stepped)


def solution(mesh):
    return jax.shard_map(
        on_device,
        mesh=mesh,
        in_specs=(P(None, None, "lat", "lon"), P(None, None, "lat", "lon"), P(), P()),
        out_specs=P(None, None, "lat", "lon"),
        check_vma=False,
    )
```

```python
import math

import jax
import jax.numpy as jnp
from jax import lax
from jax.experimental import pallas as pl
from jax.experimental.pallas import tpu as pltpu
from jax.sharding import PartitionSpec as P

KC = 256


def flip(block, axis, bit):
    count = lax.axis_size(axis)
    route = [(i, i ^ (1 << bit)) for i in range(count) if i ^ (1 << bit) < count]
    return lax.ppermute(block, axis, route)


def angle_parts(columns, circle_size):
    waves = jnp.arange(KC, dtype=jnp.int32)
    product = columns[:, None] * waves[None, :] % circle_size
    angles = product.astype(jnp.float32) * (2.0 * math.pi / circle_size)
    return jnp.cos(angles), jnp.sin(angles)


def wave_table(first, column_count, circle_size):
    fine = 32
    coarse = column_count // fine
    cos_c, sin_c = angle_parts(first + fine * jnp.arange(coarse, dtype=jnp.int32), circle_size)
    cos_f, sin_f = angle_parts(jnp.arange(fine, dtype=jnp.int32), circle_size)
    cos_c, sin_c = cos_c[:, None], sin_c[:, None]
    cos_f, sin_f = cos_f[None], sin_f[None]
    cosine = (cos_c * cos_f - sin_c * sin_f).astype(jnp.bfloat16).reshape(column_count, KC)
    sine = (sin_c * cos_f + cos_c * sin_f).astype(jnp.bfloat16).reshape(column_count, KC)
    return jnp.concatenate([cosine, sine], axis=1)


def mode_scale(cutoffs, circle_size):
    waves = jnp.arange(2 * KC, dtype=jnp.int32) % KC
    weights = jnp.where(waves == 0, 1.0 / circle_size, 2.0 / circle_size).astype(jnp.float32)
    return jnp.where(waves[None, :] <= cutoffs[:, None], weights[None, :], jnp.float32(0.0))


MESH = pl.DeviceIdType.MESH


def step_kernel(
    state,
    weights,
    table,
    stepped,
    totals,
    cells,
    planes,
    waves,
    results,
    rounded,
    top,
    bottom,
    north,
    south,
    columns_out,
    columns_in,
    sides,
    partial,
    arrived,
    load_sem,
    table_sem,
    row_send,
    row_recv,
    side_send,
    side_recv,
    sum_send,
    sum_recv,
    store_sem,
):
    chunks, fields, depth, columns = cells.shape
    size = top.shape[2]
    rows = depth // size
    half = partial.shape[1] // 2
    lat_count, lon_count = lax.axis_size("lat"), lax.axis_size("lon")
    lat, lon = lax.axis_index("lat"), lax.axis_index("lon")
    after = lax.rem(lon + 1, lon_count)
    before = lax.rem(lon + lon_count - 1, lon_count)
    across = lax.rem(lon + lon_count // 2, lon_count)
    odd = lax.rem(lon, 2)
    twin = lon + 1 - 2 * odd

    def load(g):
        part = pl.ds(pl.multiple_of(g * depth, depth), depth)
        return (
            pltpu.make_async_copy(state.at[:, part], cells.at[g], load_sem.at[0, g]),
            pltpu.make_async_copy(weights.at[:, part], planes.at[g], load_sem.at[1, g]),
        )

    def store(g):
        part = pl.ds(pl.multiple_of(g * depth, depth), depth)
        return pltpu.make_async_copy(results.at[g], stepped.at[:, part], store_sem.at[g])

    def remote(source, target, sent, got, device):
        return pltpu.make_async_remote_copy(
            src_ref=source,
            dst_ref=target,
            send_sem=sent,
            recv_sem=got,
            device_id=device,
            device_id_type=MESH,
        )

    def row_copy(g, up, device, into_north):
        return remote(
            top.at[g] if up else bottom.at[g],
            north.at[g] if into_north else south.at[g],
            row_send.at[0 if up else 1, g],
            row_recv.at[0 if into_north else 1, g],
            device,
        )

    def side_copy(k, device):
        return remote(
            columns_out.at[k], columns_in.at[k], side_send.at[k], side_recv.at[k], device
        )

    def sum_copy(g):
        away = pl.ds(pl.multiple_of((1 - odd) * half, 8), half)
        return remote(
            partial.at[g, away], arrived.at[g], sum_send.at[g], sum_recv.at[g], (lat, twin)
        )

    for g in range(chunks):
        load(g)[0].start()
    for g in range(chunks):
        load(g)[1].start()
    fetch_table = pltpu.make_async_copy(table, waves, table_sem)
    fetch_table.start()

    barrier = pltpu.get_barrier_semaphore()
    for other in (after, before, across, twin):
        pl.semaphore_signal(barrier, inc=1, device_id=(lat, other), device_id_type=MESH)

    @pl.when(lat > 0)
    def _():
        pl.semaphore_signal(barrier, inc=1, device_id=(lat - 1, lon), device_id_type=MESH)

    @pl.when(lat < lat_count - 1)
    def _():
        pl.semaphore_signal(barrier, inc=1, device_id=(lat + 1, lon), device_id_type=MESH)

    inside = (lat > 0) & (lat < lat_count - 1)

    @pl.when(inside)
    def _():
        pl.semaphore_wait(barrier, 6)

    @pl.when(jnp.logical_not(inside))
    def _():
        pl.semaphore_wait(barrier, 5)

    taker = lax.broadcasted_iota(jnp.int32, (2 * size, depth), 0)
    taken = lax.broadcasted_iota(jnp.int32, (2 * size, depth), 1)
    wanted = jnp.where(taker < size, taker * rows, (taker - size) * rows + rows - 1)
    gather = jnp.where(taken == wanted, 1.0, 0.0).astype(jnp.bfloat16)

    def send_rows(g, carry):
        load(g)[0].wait()
        for field in range(fields):
            sign = -1.0 if field < 2 else 1.0
            up_sign = jnp.where(lat == 0, sign, 1.0).astype(jnp.float32)
            down_sign = jnp.where(lat == lat_count - 1, sign, 1.0).astype(jnp.float32)
            edges = jnp.dot(
                gather,
                cells[g, field].astype(jnp.bfloat16),
                preferred_element_type=jnp.float32,
            )
            top[g, field] = (edges[:size] * up_sign).astype(jnp.bfloat16)
            bottom[g, field] = (edges[size:] * down_sign).astype(jnp.bfloat16)

        @pl.when(lat == 0)
        def _():
            row_copy(g, True, (lat, across), True).start()

        @pl.when(lat > 0)
        def _():
            row_copy(g, True, (lat - 1, lon), False).start()

        @pl.when(lat < lat_count - 1)
        def _():
            row_copy(g, False, (lat + 1, lon), True).start()

        @pl.when(lat == lat_count - 1)
        def _():
            row_copy(g, False, (lat, across), False).start()

        return carry

    lax.fori_loop(0, chunks, send_rows, 0)

    spot = lax.broadcasted_iota(jnp.int32, (16, 128), 1)
    line = lax.broadcasted_iota(jnp.int32, (16, 128), 0)

    def pick(k, lanes, lane):
        chosen = jnp.where((spot == lane) & (line == 0), 1.0, 0.0).astype(jnp.bfloat16)
        for g in range(chunks):
            for field in range(0, fields):
                first = (g * fields + field) * depth
                edge = cells[g, field, :, lanes].astype(jnp.bfloat16)
                picked = lax.dot_general(
                    chosen, edge, (((1,), (1,)), ((), ())), preferred_element_type=jnp.float32
                )
                columns_out[k, g * fields + field] = picked.astype(jnp.bfloat16)

    pick(0, pl.ds(columns - 128, 128), 127)
    side_copy(0, (lat, after)).start()
    pick(1, pl.ds(0, 128), 0)
    side_copy(1, (lat, before)).start()

    spread = jnp.where(line == 0, 1.0, 0.0).astype(jnp.bfloat16)
    for k in range(2):
        side_copy(k, (lat, after)).wait_recv()
        for at in range(chunks * fields):
            sides[k, at] = lax.dot_general(
                columns_in[k, at],
                spread,
                (((0,), (0,)), ((), ())),
                preferred_element_type=jnp.float32,
            )
    fetch_table.wait()

    lane = lax.broadcasted_iota(jnp.int32, (rows, columns), 1)
    level_line = lax.broadcasted_iota(jnp.int32, (rows, columns), 0)
    copies = columns // 128

    def one_chunk(g, carry):
        load(g)[1].wait()
        row_copy(g, True, (lat, across), True).wait_recv()
        row_copy(g, False, (lat, across), False).wait_recv()

        def one_field(field, inner):
            above = north[g, field].astype(jnp.float32)
            below = south[g, field].astype(jnp.float32)
            for level in range(0, size, 2):
                pair = []
                for at in (level, level + 1):
                    span = pl.ds(at * rows, rows)
                    x = cells[g, field, span]
                    left = jnp.concatenate([sides[0, g * fields + field, span]] * copies, axis=1)
                    right = jnp.concatenate([sides[1, g * fields + field, span]] * copies, axis=1)
                    w = jnp.where(lane == 0, left, pltpu.roll(x, 1, 1))
                    e = jnp.where(lane == columns - 1, right, pltpu.roll(x, columns - 1, 1))
                    n = jnp.where(level_line == 0, above[at : at + 1], pltpu.roll(x, 1, 0))
                    s = jnp.where(
                        level_line == rows - 1, below[at : at + 1], pltpu.roll(x, rows - 1, 0)
                    )
                    y = (
                        x
                        + planes[g, 0, span] * (e - x)
                        + planes[g, 1, span] * (w - x)
                        + planes[g, 2, span] * (n - x)
                        + planes[g, 3, span] * (s - x)
                    )
                    results[g, field, span] = y
                    pair.append(y)
                first = pl.multiple_of(field * depth + level * rows, 2 * rows)
                rounded[pl.ds(first, 2 * rows), :] = jnp.concatenate(pair, axis=0).astype(
                    jnp.bfloat16
                )
            return inner

        lax.fori_loop(0, fields, one_field, 0)
        store(g).start()
        partial[g] = jnp.dot(rounded[...], waves[...], preferred_element_type=jnp.float32)
        sum_copy(g).start()
        return carry

    lax.fori_loop(0, chunks, one_chunk, 0)

    def one_total(g, carry):
        sum_copy(g).wait_recv()
        mine = pl.ds(pl.multiple_of(odd * half, 8), half)
        totals[g] = partial[g, mine] + arrived[g]
        return carry

    lax.fori_loop(0, chunks, one_total, 0)

    def finish(g, carry):
        sum_copy(g).wait_send()
        row_copy(g, True, (lat, across), True).wait_send()
        row_copy(g, False, (lat, across), False).wait_send()
        store(g).wait()
        return carry

    lax.fori_loop(0, chunks, finish, 0)
    for k in range(2):
        side_copy(k, (lat, after)).wait_send()


def merge_kernel(keep, spectra, table, stepped, merged):
    fields, levels, rows, columns = stepped.shape
    smooth = jnp.dot(spectra[0], table[...], preferred_element_type=jnp.float32)
    smooth = smooth.astype(jnp.bfloat16).astype(jnp.float32)
    smooth = smooth.reshape(fields, levels, rows, columns)
    kept = jnp.broadcast_to(keep[...], (rows, columns)) != 0
    merged[...] = jnp.where(kept, smooth, stepped[...])


def chunk_of(fields, levels, rows, columns, size):
    return pl.BlockSpec((fields, size, rows, columns), lambda i: (0, i, 0, 0))


def whole(*shape):
    return pl.BlockSpec(shape, lambda i: (0,) * len(shape), pipeline_mode=pl.Buffered(1))


def on_device(state_fields, stencil_weights, filter_mask, cutoff_wave):
    fields, levels, rows, columns = state_fields.shape
    lat_count, lon_count = lax.axis_size("lat"), lax.axis_size("lon")
    lat_pos, lon_pos = lax.axis_index("lat"), lax.axis_index("lon")
    circle_size = columns * lon_count
    bits = lon_count.bit_length() - 1
    size = 8
    steps = levels // size
    start = lat_pos * rows
    cuts = lax.dynamic_slice_in_dim(cutoff_wave, start, rows)
    mask = lax.dynamic_slice_in_dim(filter_mask, start, rows)
    table = wave_table(lon_pos * columns, columns, circle_size)
    rows_each = fields * size * rows
    depth = size * rows
    anywhere = pl.BlockSpec(memory_space=pl.ANY)
    dma = pltpu.SemaphoreType.DMA
    strip = pltpu.VMEM((steps, fields, size, columns), jnp.bfloat16)
    column_strip = pltpu.VMEM((2, steps * fields, 16, depth), jnp.bfloat16)
    stepped, total = pl.pallas_call(
        step_kernel,
        in_specs=[anywhere] * 3,
        out_specs=[anywhere, pl.BlockSpec(memory_space=pltpu.VMEM)],
        out_shape=[
            jax.ShapeDtypeStruct((fields, levels * rows, columns), jnp.float32),
            jax.ShapeDtypeStruct((steps, rows_each // 2, 2 * KC), jnp.float32),
        ],
        scratch_shapes=[
            pltpu.VMEM((steps, fields, depth, columns), jnp.float32),
            pltpu.VMEM((steps, 4, depth, columns), jnp.float32),
            pltpu.VMEM((columns, 2 * KC), jnp.bfloat16),
            pltpu.VMEM((steps, fields, depth, columns), jnp.float32),
            pltpu.VMEM((rows_each, columns), jnp.bfloat16),
            strip,
            strip,
            strip,
            strip,
            column_strip,
            column_strip,
            pltpu.VMEM((2, steps * fields, depth, 128), jnp.float32),
            pltpu.VMEM((steps, rows_each, 2 * KC), jnp.float32),
            pltpu.VMEM((steps, rows_each // 2, 2 * KC), jnp.float32),
            dma((2, steps)),
            dma,
            dma((2, steps)),
            dma((2, steps)),
            dma((2,)),
            dma((2,)),
            dma((steps,)),
            dma((steps,)),
            dma((steps,)),
        ],
        compiler_params=pltpu.CompilerParams(collective_id=0, has_side_effects=True),
        name="step",
    )(
        state_fields.reshape(fields, levels * rows, columns),
        stencil_weights.reshape(4, levels * rows, columns),
        table,
    )
    stepped = stepped.reshape(state_fields.shape)
    low = lon_pos % 2 == 0
    for bit in range(1, bits):
        total = total + flip(total.astype(jnp.float16), "lon", bit).astype(jnp.float32)
    scale = mode_scale(cuts, circle_size)
    spectra = (total.reshape(steps, -1, rows, 2 * KC) * scale).astype(jnp.bfloat16)
    spectra = spectra.reshape(steps, -1, 2 * KC)
    other = flip(spectra, "lon", 0)
    spectra = jnp.concatenate(
        [jnp.where(low, spectra, other), jnp.where(low, other, spectra)], axis=1
    )
    back_table = table.T
    return pl.pallas_call(
        merge_kernel,
        grid=(steps,),
        in_specs=[
            whole(rows, 1),
            pl.BlockSpec((1, rows_each, 2 * KC), lambda i: (i, 0, 0)),
            whole(2 * KC, columns),
            chunk_of(fields, levels, rows, columns, size),
        ],
        out_specs=chunk_of(fields, levels, rows, columns, size),
        out_shape=jax.ShapeDtypeStruct(state_fields.shape, jnp.float32),
        name="merge",
    )(mask[:, None], spectra, back_table, stepped)


def solution(mesh):
    return jax.shard_map(
        on_device,
        mesh=mesh,
        in_specs=(P(None, None, "lat", "lon"), P(None, None, "lat", "lon"), P(), P()),
        out_specs=P(None, None, "lat", "lon"),
        check_vma=False,
    )
```

```python
import math

import jax
import jax.numpy as jnp
from jax import lax
from jax.experimental import pallas as pl
from jax.experimental.pallas import tpu as pltpu
from jax.sharding import PartitionSpec as P

KC = 256


def angle_parts(columns, circle_size, axis):
    waves = lax.broadcasted_iota(
        jnp.int32, (columns.size, KC) if axis == 1 else (KC, columns.size), axis
    )
    product = jnp.expand_dims(columns, axis) * waves % circle_size
    angles = product.astype(jnp.float32) * (2.0 * math.pi / circle_size)
    return jnp.cos(angles), jnp.sin(angles)


def mode_scale(cutoffs, circle_size):
    waves = jnp.arange(2 * KC, dtype=jnp.int32) % KC
    weights = jnp.where(waves == 0, 1.0 / circle_size, 2.0 / circle_size).astype(jnp.float32)
    return jnp.where(waves[None, :] <= cutoffs[:, None], weights[None, :], jnp.float32(0.0))


MESH = pl.DeviceIdType.MESH


def step_kernel(
    state,
    weights,
    cosines,
    sines,
    turned_cosines,
    turned_sines,
    scale,
    keep,
    stepped,
    cells,
    planes,
    waves,
    turned,
    results,
    rounded,
    top,
    bottom,
    north,
    south,
    columns_out,
    columns_in,
    sides,
    partial,
    halves,
    quarters,
    half_in,
    quarter_in,
    spectra,
    load_sem,
    row_send,
    row_recv,
    side_send,
    side_recv,
    sum_send,
    sum_recv,
    join_send,
    join_recv,
    store_sem,
):
    chunks, fields, depth, columns = cells.shape
    size = top.shape[2]
    rows = depth // size
    modes = waves.shape[1] // 2
    half = partial.shape[1] // 2
    quarter = half // 2
    lat_count, lon_count = lax.axis_size("lat"), lax.axis_size("lon")
    lat, lon = lax.axis_index("lat"), lax.axis_index("lon")
    after = lax.rem(lon + 1, lon_count)
    before = lax.rem(lon + lon_count - 1, lon_count)
    across = lax.rem(lon + lon_count // 2, lon_count)
    bits = lon_count.bit_length() - 1
    digit = [lax.rem(lon // (1 << b), 2) for b in range(bits)]
    peer = [lon + (1 << b) - (2 << b) * digit[b] for b in range(bits)]
    own_half = digit[0] * half
    own_quarter = digit[1] * quarter

    def load(g):
        part = pl.ds(pl.multiple_of(g * depth, depth), depth)
        return (
            pltpu.make_async_copy(state.at[:, part], cells.at[g], load_sem.at[0, g]),
            pltpu.make_async_copy(weights.at[:, part], planes.at[g], load_sem.at[1, g]),
        )

    def store(g):
        part = pl.ds(pl.multiple_of(g * depth, depth), depth)
        return pltpu.make_async_copy(results.at[g], stepped.at[:, part], store_sem.at[g])

    def remote(source, target, sent, got, device):
        return pltpu.make_async_remote_copy(
            src_ref=source,
            dst_ref=target,
            send_sem=sent,
            recv_sem=got,
            device_id=device,
            device_id_type=MESH,
        )

    def row_copy(g, up, device, into_north):
        return remote(
            top.at[g] if up else bottom.at[g],
            north.at[g] if into_north else south.at[g],
            row_send.at[0 if up else 1, g],
            row_recv.at[0 if into_north else 1, g],
            device,
        )

    def side_copy(k, device):
        return remote(
            columns_out.at[k], columns_in.at[k], side_send.at[k], side_recv.at[k], device
        )

    def sum_copy(b, g):
        if b == 0:
            away = pl.ds(pl.multiple_of((1 - digit[0]) * half, 16), half)
            source, target = partial.at[g, away], half_in.at[g]
        elif b == 1:
            away = pl.ds(pl.multiple_of((1 - digit[1]) * quarter, 16), quarter)
            source, target = halves.at[g, away], quarter_in.at[0, g]
        else:
            source, target = quarters.at[b - 2, g], quarter_in.at[b - 1, g]
        return remote(source, target, sum_send.at[b, g], sum_recv.at[b, g], (lat, peer[b]))

    def join_copy(b, g):
        if b == 0:
            part = pl.ds(pl.multiple_of(own_half, 16), half)
        else:
            part = pl.ds(pl.multiple_of(own_half + own_quarter, 16), quarter)
        view = spectra.at[g, part]
        return remote(view, view, join_send.at[b, g], join_recv.at[b, g], (lat, peer[b]))

    for g in range(chunks):
        load(g)[0].start()
    for g in range(chunks):
        load(g)[1].start()

    barrier = pltpu.get_barrier_semaphore()
    for other in (after, before, across, *peer):
        pl.semaphore_signal(barrier, inc=1, device_id=(lat, other), device_id_type=MESH)

    @pl.when(lat > 0)
    def _():
        pl.semaphore_signal(barrier, inc=1, device_id=(lat - 1, lon), device_id_type=MESH)

    @pl.when(lat < lat_count - 1)
    def _():
        pl.semaphore_signal(barrier, inc=1, device_id=(lat + 1, lon), device_id_type=MESH)

    inside = (lat > 0) & (lat < lat_count - 1)

    @pl.when(inside)
    def _():
        pl.semaphore_wait(barrier, 5 + bits)

    @pl.when(jnp.logical_not(inside))
    def _():
        pl.semaphore_wait(barrier, 4 + bits)

    taker = lax.broadcasted_iota(jnp.int32, (2 * size, depth), 0)
    taken = lax.broadcasted_iota(jnp.int32, (2 * size, depth), 1)
    wanted = jnp.where(taker < size, taker * rows, (taker - size) * rows + rows - 1)
    gather = jnp.where(taken == wanted, 1.0, 0.0).astype(jnp.bfloat16)

    def send_rows(g, carry):
        load(g)[0].wait()
        for field in range(fields):
            sign = -1.0 if field < 2 else 1.0
            up_sign = jnp.where(lat == 0, sign, 1.0).astype(jnp.float32)
            down_sign = jnp.where(lat == lat_count - 1, sign, 1.0).astype(jnp.float32)
            edges = jnp.dot(
                gather,
                cells[g, field].astype(jnp.bfloat16),
                preferred_element_type=jnp.float32,
            )
            top[g, field] = (edges[:size] * up_sign).astype(jnp.bfloat16)
            bottom[g, field] = (edges[size:] * down_sign).astype(jnp.bfloat16)

        @pl.when(lat == 0)
        def _():
            row_copy(g, True, (lat, across), True).start()

        @pl.when(lat > 0)
        def _():
            row_copy(g, True, (lat - 1, lon), False).start()

        @pl.when(lat < lat_count - 1)
        def _():
            row_copy(g, False, (lat + 1, lon), True).start()

        @pl.when(lat == lat_count - 1)
        def _():
            row_copy(g, False, (lat, across), False).start()

        return carry

    lax.fori_loop(0, chunks, send_rows, 0)

    spot = lax.broadcasted_iota(jnp.int32, (16, 128), 1)
    line = lax.broadcasted_iota(jnp.int32, (16, 128), 0)

    def pick(k, lanes, lane):
        chosen = jnp.where((spot == lane) & (line == 0), 1.0, 0.0).astype(jnp.bfloat16)
        for g in range(chunks):
            for field in range(0, fields):
                first = (g * fields + field) * depth
                edge = cells[g, field, :, lanes].astype(jnp.bfloat16)
                picked = lax.dot_general(
                    chosen, edge, (((1,), (1,)), ((), ())), preferred_element_type=jnp.float32
                )
                columns_out[k, g * fields + field] = picked.astype(jnp.bfloat16)

    pick(0, pl.ds(columns - 128, 128), 127)
    side_copy(0, (lat, after)).start()
    pick(1, pl.ds(0, 128), 0)
    side_copy(1, (lat, before)).start()

    fine = 32
    coarse = columns // fine
    fine_cos, fine_sin = cosines[coarse:], sines[coarse:]

    def fill(at, carry):
        span = pl.ds(pl.multiple_of(at * fine, fine), fine)
        coarse_cos, coarse_sin = cosines[pl.ds(at, 1)], sines[pl.ds(at, 1)]
        waves[span, :modes] = (coarse_cos * fine_cos - coarse_sin * fine_sin).astype(jnp.bfloat16)
        waves[span, modes:] = (coarse_sin * fine_cos + coarse_cos * fine_sin).astype(jnp.bfloat16)
        return carry

    lax.fori_loop(0, coarse, fill, 0)
    lane_cos, lane_sin = turned_cosines[:, :128], turned_sines[:, :128]
    for at in range(columns // 128):
        span = pl.ds(at * 128, 128)
        tile_cos = turned_cosines[:, 128 + at : 129 + at]
        tile_sin = turned_sines[:, 128 + at : 129 + at]
        turned[:modes, span] = (tile_cos * lane_cos - tile_sin * lane_sin).astype(jnp.bfloat16)
        turned[modes:, span] = (tile_sin * lane_cos + tile_cos * lane_sin).astype(jnp.bfloat16)

    spread = jnp.where(line == 0, 1.0, 0.0).astype(jnp.bfloat16)
    for k in range(2):
        side_copy(k, (lat, after)).wait_recv()
        for at in range(chunks * fields):
            sides[k, at] = lax.dot_general(
                columns_in[k, at],
                spread,
                (((0,), (0,)), ((), ())),
                preferred_element_type=jnp.float32,
            )

    lane = lax.broadcasted_iota(jnp.int32, (rows, columns), 1)
    level_line = lax.broadcasted_iota(jnp.int32, (rows, columns), 0)
    copies = columns // 128

    def advance(g):
        load(g)[1].wait()
        row_copy(g, True, (lat, across), True).wait_recv()
        row_copy(g, False, (lat, across), False).wait_recv()

        def one_field(field, inner):
            above = north[g, field].astype(jnp.float32)
            below = south[g, field].astype(jnp.float32)
            for level in range(0, size, 2):
                pair = []
                for at in (level, level + 1):
                    span = pl.ds(at * rows, rows)
                    x = cells[g, field, span]
                    left = jnp.concatenate([sides[0, g * fields + field, span]] * copies, axis=1)
                    right = jnp.concatenate([sides[1, g * fields + field, span]] * copies, axis=1)
                    w = jnp.where(lane == 0, left, pltpu.roll(x, 1, 1))
                    e = jnp.where(lane == columns - 1, right, pltpu.roll(x, columns - 1, 1))
                    n = jnp.where(level_line == 0, above[at : at + 1], pltpu.roll(x, 1, 0))
                    s = jnp.where(
                        level_line == rows - 1, below[at : at + 1], pltpu.roll(x, rows - 1, 0)
                    )
                    y = (
                        x
                        + planes[g, 0, span] * (e - x)
                        + planes[g, 1, span] * (w - x)
                        + planes[g, 2, span] * (n - x)
                        + planes[g, 3, span] * (s - x)
                    )
                    results[g, field, span] = y
                    pair.append(y)
                first = pl.multiple_of(field * depth + level * rows, 2 * rows)
                rounded[pl.ds(first, 2 * rows), :] = jnp.concatenate(pair, axis=0).astype(
                    jnp.bfloat16
                )
            return inner

        lax.fori_loop(0, fields, one_field, 0)
        partial[g] = jnp.dot(rounded[...], waves[...], preferred_element_type=jnp.float32)
        sum_copy(0, g).start()

    def pair_sum(g):
        sum_copy(0, g).wait_recv()
        mine = pl.ds(pl.multiple_of(own_half, 16), half)
        halves[g] = partial[g, mine] + half_in[g]
        sum_copy(1, g).start()

    def full_sum(g):
        sum_copy(1, g).wait_recv()
        mine = pl.ds(pl.multiple_of(own_quarter, 16), quarter)
        total = halves[g, mine] + quarter_in[0, g]
        for b in range(2, bits):
            quarters[b - 2, g] = total
            sum_copy(b, g).start()
            sum_copy(b, g).wait_recv()
            total = total + quarter_in[b - 1, g]
        scaled = total.reshape(quarter // rows, rows, 2 * modes) * scale[...]
        part = pl.ds(pl.multiple_of(own_half + own_quarter, 16), quarter)
        spectra[g, part] = scaled.reshape(quarter, 2 * modes).astype(jnp.bfloat16)
        join_copy(1, g).start()

    def join(g):
        join_copy(1, g).wait_recv()
        join_copy(0, g).start()

    def merge(g):
        join_copy(0, g).wait_recv()
        smooth = jnp.dot(spectra[g], turned[...], preferred_element_type=jnp.float32)
        smooth = smooth.astype(jnp.bfloat16).astype(jnp.float32)
        smooth = smooth.reshape(fields, size, rows, columns)
        kept = jnp.broadcast_to(keep[...], (rows, columns)) != 0
        for field in range(fields):
            for at in range(size):
                span = pl.ds(at * rows, rows)
                results[g, field, span] = jnp.where(
                    kept, smooth[field, at], results[g, field, span]
                )
        store(g).start()

    def phase(t, carry):
        @pl.when(t < chunks)
        def _():
            advance(t)

        @pl.when((t >= 1) & (t <= chunks))
        def _():
            full_sum(t - 1)

        @pl.when(t >= 3)
        def _():
            merge(t - 3)

        @pl.when((t >= 2) & (t <= chunks + 1))
        def _():
            join(t - 2)

        @pl.when(t < chunks)
        def _():
            pair_sum(t)

        return carry

    lax.fori_loop(0, chunks + 3, phase, 0)

    def finish(g, carry):
        for b in range(bits):
            sum_copy(b, g).wait_send()
        for b in range(2):
            join_copy(b, g).wait_send()
        row_copy(g, True, (lat, across), True).wait_send()
        row_copy(g, False, (lat, across), False).wait_send()
        store(g).wait()
        return carry

    lax.fori_loop(0, chunks, finish, 0)
    for k in range(2):
        side_copy(k, (lat, after)).wait_send()


def on_device(state_fields, stencil_weights, filter_mask, cutoff_wave):
    fields, levels, rows, columns = state_fields.shape
    lat_count, lon_count = lax.axis_size("lat"), lax.axis_size("lon")
    lat_pos, lon_pos = lax.axis_index("lat"), lax.axis_index("lon")
    circle_size = columns * lon_count
    size = 8
    steps = levels // size
    start = lat_pos * rows
    cuts = lax.dynamic_slice_in_dim(cutoff_wave, start, rows)
    mask = lax.dynamic_slice_in_dim(filter_mask, start, rows)
    scale = mode_scale(cuts, circle_size)
    origin = lon_pos * columns
    cosines, sines = angle_parts(
        jnp.concatenate(
            [origin + 32 * jnp.arange(columns // 32), jnp.arange(32)]
        ).astype(jnp.int32),
        circle_size,
        1,
    )
    turned_cosines, turned_sines = angle_parts(
        jnp.concatenate(
            [jnp.arange(128), origin + 128 * jnp.arange(columns // 128)]
        ).astype(jnp.int32),
        circle_size,
        0,
    )
    rows_each = fields * size * rows
    depth = size * rows
    anywhere = pl.BlockSpec(memory_space=pl.ANY)
    dma = pltpu.SemaphoreType.DMA
    strip = pltpu.VMEM((steps, fields, size, columns), jnp.bfloat16)
    column_strip = pltpu.VMEM((2, steps * fields, 16, depth), jnp.bfloat16)
    extra = max(lon_count.bit_length() - 3, 1)
    in_vmem = pl.BlockSpec(memory_space=pltpu.VMEM)
    bits = lon_count.bit_length() - 1
    advanced = pl.pallas_call(
        step_kernel,
        in_specs=[anywhere] * 2 + [in_vmem] * 6,
        out_specs=anywhere,
        out_shape=jax.ShapeDtypeStruct((fields, levels * rows, columns), jnp.float32),
        scratch_shapes=[
            pltpu.VMEM((steps, fields, depth, columns), jnp.float32),
            pltpu.VMEM((steps, 4, depth, columns), jnp.float32),
            pltpu.VMEM((columns, 2 * KC), jnp.bfloat16),
            pltpu.VMEM((2 * KC, columns), jnp.bfloat16),
            pltpu.VMEM((steps, fields, depth, columns), jnp.float32),
            pltpu.VMEM((rows_each, columns), jnp.bfloat16),
            strip,
            strip,
            strip,
            strip,
            column_strip,
            column_strip,
            pltpu.VMEM((2, steps * fields, depth, 128), jnp.float32),
            pltpu.VMEM((steps, rows_each, 2 * KC), jnp.float32),
            pltpu.VMEM((steps, rows_each // 2, 2 * KC), jnp.float32),
            pltpu.VMEM((extra, steps, rows_each // 4, 2 * KC), jnp.float32),
            pltpu.VMEM((steps, rows_each // 2, 2 * KC), jnp.float32),
            pltpu.VMEM((bits - 1, steps, rows_each // 4, 2 * KC), jnp.float32),
            pltpu.VMEM((steps, rows_each, 2 * KC), jnp.bfloat16),
            dma((2, steps)),
            dma((2, steps)),
            dma((2, steps)),
            dma((2,)),
            dma((2,)),
            dma((bits, steps)),
            dma((bits, steps)),
            dma((2, steps)),
            dma((2, steps)),
            dma((steps,)),
        ],
        compiler_params=pltpu.CompilerParams(
            collective_id=0, has_side_effects=True, vmem_limit_bytes=60 << 20
        ),
        name="step",
    )(
        state_fields.reshape(fields, levels * rows, columns),
        stencil_weights.reshape(4, levels * rows, columns),
        cosines,
        sines,
        turned_cosines,
        turned_sines,
        scale,
        mask[:, None],
    )
    return advanced.reshape(state_fields.shape)


def solution(mesh):
    return jax.shard_map(
        on_device,
        mesh=mesh,
        in_specs=(P(None, None, "lat", "lon"), P(None, None, "lat", "lon"), P(), P()),
        out_specs=P(None, None, "lat", "lon"),
        check_vma=False,
    )
```

```python
import math

import jax
import jax.numpy as jnp
from jax import lax
from jax.experimental import pallas as pl
from jax.experimental.pallas import tpu as pltpu
from jax.sharding import PartitionSpec as P

KC = 256


def angle_parts(columns, circle_size, axis):
    waves = lax.broadcasted_iota(
        jnp.int32, (columns.size, KC) if axis == 1 else (KC, columns.size), axis
    )
    product = jnp.expand_dims(columns, axis) * waves % circle_size
    angles = product.astype(jnp.float32) * (2.0 * math.pi / circle_size)
    return jnp.cos(angles), jnp.sin(angles)


MESH = pl.DeviceIdType.MESH


def step_kernel(
    state,
    weights,
    cosines,
    sines,
    turned_cosines,
    turned_sines,
    bounds,
    stepped,
    cells,
    planes,
    waves,
    turned,
    results,
    rounded,
    top,
    bottom,
    north,
    south,
    columns_out,
    columns_in,
    sides,
    partial,
    halves,
    quarters,
    half_in,
    quarter_in,
    spectra,
    load_sem,
    row_send,
    row_recv,
    side_send,
    side_recv,
    sum_send,
    sum_recv,
    join_send,
    join_recv,
    store_sem,
):
    chunks, fields, depth, columns = cells.shape
    size = top.shape[2]
    rows = depth // size
    modes = waves.shape[1] // 2
    half = partial.shape[1] // 2
    quarter = half // 2
    lat_count, lon_count = lax.axis_size("lat"), lax.axis_size("lon")
    lat, lon = lax.axis_index("lat"), lax.axis_index("lon")
    after = lax.rem(lon + 1, lon_count)
    before = lax.rem(lon + lon_count - 1, lon_count)
    across = lax.rem(lon + lon_count // 2, lon_count)
    bits = lon_count.bit_length() - 1
    digit = [lax.rem(lon // (1 << b), 2) for b in range(bits)]
    peer = [lon + (1 << b) - (2 << b) * digit[b] for b in range(bits)]
    own_half = digit[0] * half
    own_quarter = digit[1] * quarter

    def load(g):
        part = pl.ds(pl.multiple_of(g * depth, depth), depth)
        return (
            pltpu.make_async_copy(state.at[:, part], cells.at[g], load_sem.at[0, g]),
            pltpu.make_async_copy(weights.at[:, part], planes.at[g], load_sem.at[1, g]),
        )

    def store(g):
        part = pl.ds(pl.multiple_of(g * depth, depth), depth)
        return pltpu.make_async_copy(results.at[g], stepped.at[:, part], store_sem.at[g])

    def remote(source, target, sent, got, device):
        return pltpu.make_async_remote_copy(
            src_ref=source,
            dst_ref=target,
            send_sem=sent,
            recv_sem=got,
            device_id=device,
            device_id_type=MESH,
        )

    def row_copy(g, up, device, into_north):
        return remote(
            top.at[g] if up else bottom.at[g],
            north.at[g] if into_north else south.at[g],
            row_send.at[0 if up else 1, g],
            row_recv.at[0 if into_north else 1, g],
            device,
        )

    def side_copy(k, device):
        return remote(
            columns_out.at[k], columns_in.at[k], side_send.at[k], side_recv.at[k], device
        )

    def sum_copy(b, g):
        if b == 0:
            away = pl.ds(pl.multiple_of((1 - digit[0]) * half, 16), half)
            source, target = partial.at[g, away], half_in.at[g]
        elif b == 1:
            away = pl.ds(pl.multiple_of((1 - digit[1]) * quarter, 16), quarter)
            source, target = halves.at[g, away], quarter_in.at[0, g]
        else:
            source, target = quarters.at[b - 2, g], quarter_in.at[b - 1, g]
        return remote(source, target, sum_send.at[b, g], sum_recv.at[b, g], (lat, peer[b]))

    def join_copy(b, g):
        if b == 0:
            part = pl.ds(pl.multiple_of(own_half, 16), half)
        else:
            part = pl.ds(pl.multiple_of(own_half + own_quarter, 16), quarter)
        view = spectra.at[g, part]
        return remote(view, view, join_send.at[b, g], join_recv.at[b, g], (lat, peer[b]))

    for g in range(chunks):
        load(g)[0].start()
    for g in range(chunks):
        load(g)[1].start()

    barrier = pltpu.get_barrier_semaphore()
    for other in (after, before, across, *peer):
        pl.semaphore_signal(barrier, inc=1, device_id=(lat, other), device_id_type=MESH)

    @pl.when(lat > 0)
    def _():
        pl.semaphore_signal(barrier, inc=1, device_id=(lat - 1, lon), device_id_type=MESH)

    @pl.when(lat < lat_count - 1)
    def _():
        pl.semaphore_signal(barrier, inc=1, device_id=(lat + 1, lon), device_id_type=MESH)

    inside = (lat > 0) & (lat < lat_count - 1)

    @pl.when(inside)
    def _():
        pl.semaphore_wait(barrier, 5 + bits)

    @pl.when(jnp.logical_not(inside))
    def _():
        pl.semaphore_wait(barrier, 4 + bits)

    taker = lax.broadcasted_iota(jnp.int32, (2 * size, depth), 0)
    taken = lax.broadcasted_iota(jnp.int32, (2 * size, depth), 1)
    wanted = jnp.where(taker < size, taker * rows, (taker - size) * rows + rows - 1)
    gather = jnp.where(taken == wanted, 1.0, 0.0).astype(jnp.bfloat16)

    def send_rows(g, carry):
        load(g)[0].wait()
        for field in range(fields):
            sign = -1.0 if field < 2 else 1.0
            up_sign = jnp.where(lat == 0, sign, 1.0).astype(jnp.float32)
            down_sign = jnp.where(lat == lat_count - 1, sign, 1.0).astype(jnp.float32)
            edges = jnp.dot(
                gather,
                cells[g, field].astype(jnp.bfloat16),
                preferred_element_type=jnp.float32,
            )
            top[g, field] = (edges[:size] * up_sign).astype(jnp.bfloat16)
            bottom[g, field] = (edges[size:] * down_sign).astype(jnp.bfloat16)

        @pl.when(lat == 0)
        def _():
            row_copy(g, True, (lat, across), True).start()

        @pl.when(lat > 0)
        def _():
            row_copy(g, True, (lat - 1, lon), False).start()

        @pl.when(lat < lat_count - 1)
        def _():
            row_copy(g, False, (lat + 1, lon), True).start()

        @pl.when(lat == lat_count - 1)
        def _():
            row_copy(g, False, (lat, across), False).start()

        return carry

    lax.fori_loop(0, chunks, send_rows, 0)

    spot = lax.broadcasted_iota(jnp.int32, (16, 128), 1)
    line = lax.broadcasted_iota(jnp.int32, (16, 128), 0)

    def pick(k, lanes, lane):
        chosen = jnp.where((spot == lane) & (line == 0), 1.0, 0.0).astype(jnp.bfloat16)
        for g in range(chunks):
            for field in range(0, fields):
                first = (g * fields + field) * depth
                edge = cells[g, field, :, lanes].astype(jnp.bfloat16)
                picked = lax.dot_general(
                    chosen, edge, (((1,), (1,)), ((), ())), preferred_element_type=jnp.float32
                )
                columns_out[k, g * fields + field] = picked.astype(jnp.bfloat16)

    pick(0, pl.ds(columns - 128, 128), 127)
    side_copy(0, (lat, after)).start()
    pick(1, pl.ds(0, 128), 0)
    side_copy(1, (lat, before)).start()

    fine = 32
    coarse = columns // fine
    fine_cos, fine_sin = cosines[coarse:], sines[coarse:]

    def fill(at, carry):
        span = pl.ds(pl.multiple_of(at * fine, fine), fine)
        coarse_cos, coarse_sin = cosines[pl.ds(at, 1)], sines[pl.ds(at, 1)]
        waves[span, :modes] = (coarse_cos * fine_cos - coarse_sin * fine_sin).astype(jnp.bfloat16)
        waves[span, modes:] = (coarse_sin * fine_cos + coarse_cos * fine_sin).astype(jnp.bfloat16)
        return carry

    lax.fori_loop(0, coarse, fill, 0)
    lane_cos, lane_sin = turned_cosines[:, :128], turned_sines[:, :128]
    for at in range(columns // 128):
        span = pl.ds(at * 128, 128)
        tile_cos = turned_cosines[:, 128 + at : 129 + at]
        tile_sin = turned_sines[:, 128 + at : 129 + at]
        turned[:modes, span] = (tile_cos * lane_cos - tile_sin * lane_sin).astype(jnp.bfloat16)
        turned[modes:, span] = (tile_sin * lane_cos + tile_cos * lane_sin).astype(jnp.bfloat16)

    spread = jnp.where(line == 0, 1.0, 0.0).astype(jnp.bfloat16)
    for k in range(2):
        side_copy(k, (lat, after)).wait_recv()
        for at in range(chunks * fields):
            sides[k, at] = lax.dot_general(
                columns_in[k, at],
                spread,
                (((0,), (0,)), ((), ())),
                preferred_element_type=jnp.float32,
            )

    lane = lax.broadcasted_iota(jnp.int32, (rows, columns), 1)
    level_line = lax.broadcasted_iota(jnp.int32, (rows, columns), 0)
    copies = columns // 128

    wave = lax.rem(lax.broadcasted_iota(jnp.int32, (rows, 2 * modes), 1), modes)
    circle_size = columns * lon_count
    weight = jnp.where(wave == 0, 1.0 / circle_size, 2.0 / circle_size)
    scale = jnp.where(wave <= bounds[:, 1:2], weight, 0.0).astype(jnp.float32)

    def advance(g):
        load(g)[1].wait()
        row_copy(g, True, (lat, across), True).wait_recv()
        row_copy(g, False, (lat, across), False).wait_recv()

        def one_field(field, inner):
            above = north[g, field].astype(jnp.float32)
            below = south[g, field].astype(jnp.float32)
            for level in range(0, size, 2):
                pair = []
                for at in (level, level + 1):
                    span = pl.ds(at * rows, rows)
                    x = cells[g, field, span]
                    left = jnp.concatenate([sides[0, g * fields + field, span]] * copies, axis=1)
                    right = jnp.concatenate([sides[1, g * fields + field, span]] * copies, axis=1)
                    w = jnp.where(lane == 0, left, pltpu.roll(x, 1, 1))
                    e = jnp.where(lane == columns - 1, right, pltpu.roll(x, columns - 1, 1))
                    n = jnp.where(level_line == 0, above[at : at + 1], pltpu.roll(x, 1, 0))
                    s = jnp.where(
                        level_line == rows - 1, below[at : at + 1], pltpu.roll(x, rows - 1, 0)
                    )
                    y = (
                        x
                        + planes[g, 0, span] * (e - x)
                        + planes[g, 1, span] * (w - x)
                        + planes[g, 2, span] * (n - x)
                        + planes[g, 3, span] * (s - x)
                    )
                    results[g, field, span] = y
                    pair.append(y)
                first = pl.multiple_of(field * depth + level * rows, 2 * rows)
                rounded[pl.ds(first, 2 * rows), :] = jnp.concatenate(pair, axis=0).astype(
                    jnp.bfloat16
                )
            return inner

        lax.fori_loop(0, fields, one_field, 0)
        partial[g] = jnp.dot(rounded[...], waves[...], preferred_element_type=jnp.float32)
        sum_copy(0, g).start()

    def pair_sum(g):
        sum_copy(0, g).wait_recv()
        mine = pl.ds(pl.multiple_of(own_half, 16), half)
        halves[g] = partial[g, mine] + half_in[g]
        sum_copy(1, g).start()

    def full_sum(g):
        sum_copy(1, g).wait_recv()
        mine = pl.ds(pl.multiple_of(own_quarter, 16), quarter)
        total = halves[g, mine] + quarter_in[0, g]
        for b in range(2, bits):
            quarters[b - 2, g] = total
            sum_copy(b, g).start()
            sum_copy(b, g).wait_recv()
            total = total + quarter_in[b - 1, g]
        scaled = total.reshape(quarter // rows, rows, 2 * modes) * scale[None]
        part = pl.ds(pl.multiple_of(own_half + own_quarter, 16), quarter)
        spectra[g, part] = scaled.reshape(quarter, 2 * modes).astype(jnp.bfloat16)
        join_copy(1, g).start()

    def join(g):
        join_copy(1, g).wait_recv()
        join_copy(0, g).start()

    def merge(g):
        join_copy(0, g).wait_recv()
        smooth = jnp.dot(spectra[g], turned[...], preferred_element_type=jnp.float32)
        smooth = smooth.astype(jnp.bfloat16).astype(jnp.float32)
        smooth = smooth.reshape(fields, size, rows, columns)
        kept = jnp.broadcast_to(bounds[:, 0:1], (rows, columns)) != 0
        for field in range(fields):
            for at in range(size):
                span = pl.ds(at * rows, rows)
                results[g, field, span] = jnp.where(
                    kept, smooth[field, at], results[g, field, span]
                )
        store(g).start()

    def forward(t, carry):
        advance(t)

        @pl.when(t >= 1)
        def _():
            pair_sum(t - 1)

        return carry

    last = chunks - 1
    lax.fori_loop(0, chunks, forward, 0)
    full_sum(0)
    pair_sum(last)

    def sums(g, carry):
        full_sum(g)
        return carry

    def joins(g, carry):
        join(g)
        return carry

    def merges(g, carry):
        merge(g)

        @pl.when(g + 2 < chunks)
        def _():
            join(g + 2)

        return carry

    lax.fori_loop(1, last, sums, 0)
    lax.fori_loop(0, 2, joins, 0)
    full_sum(last)
    lax.fori_loop(0, chunks, merges, 0)

    def finish(g, carry):
        for b in range(bits):
            sum_copy(b, g).wait_send()
        for b in range(2):
            join_copy(b, g).wait_send()
        row_copy(g, True, (lat, across), True).wait_send()
        row_copy(g, False, (lat, across), False).wait_send()
        store(g).wait()
        return carry

    lax.fori_loop(0, chunks, finish, 0)
    for k in range(2):
        side_copy(k, (lat, after)).wait_send()


def on_device(state_fields, stencil_weights, filter_mask, cutoff_wave):
    fields, levels, rows, columns = state_fields.shape
    lat_count, lon_count = lax.axis_size("lat"), lax.axis_size("lon")
    lat_pos, lon_pos = lax.axis_index("lat"), lax.axis_index("lon")
    circle_size = columns * lon_count
    size = 8
    steps = levels // size
    start = lat_pos * rows
    bounds = lax.dynamic_slice_in_dim(jnp.stack([filter_mask, cutoff_wave], axis=1), start, rows)
    origin = lon_pos * columns
    cosines, sines = angle_parts(
        jnp.concatenate(
            [origin + 32 * jnp.arange(columns // 32), jnp.arange(32)]
        ).astype(jnp.int32),
        circle_size,
        1,
    )
    turned_cosines, turned_sines = angle_parts(
        jnp.concatenate(
            [jnp.arange(128), origin + 128 * jnp.arange(columns // 128)]
        ).astype(jnp.int32),
        circle_size,
        0,
    )
    rows_each = fields * size * rows
    depth = size * rows
    anywhere = pl.BlockSpec(memory_space=pl.ANY)
    dma = pltpu.SemaphoreType.DMA
    strip = pltpu.VMEM((steps, fields, size, columns), jnp.bfloat16)
    column_strip = pltpu.VMEM((2, steps * fields, 16, depth), jnp.bfloat16)
    extra = max(lon_count.bit_length() - 3, 1)
    in_vmem = pl.BlockSpec(memory_space=pltpu.VMEM)
    bits = lon_count.bit_length() - 1
    advanced = pl.pallas_call(
        step_kernel,
        in_specs=[anywhere] * 2 + [in_vmem] * 5,
        out_specs=anywhere,
        out_shape=jax.ShapeDtypeStruct((fields, levels * rows, columns), jnp.float32),
        scratch_shapes=[
            pltpu.VMEM((steps, fields, depth, columns), jnp.float32),
            pltpu.VMEM((steps, 4, depth, columns), jnp.float32),
            pltpu.VMEM((columns, 2 * KC), jnp.bfloat16),
            pltpu.VMEM((2 * KC, columns), jnp.bfloat16),
            pltpu.VMEM((steps, fields, depth, columns), jnp.float32),
            pltpu.VMEM((rows_each, columns), jnp.bfloat16),
            strip,
            strip,
            strip,
            strip,
            column_strip,
            column_strip,
            pltpu.VMEM((2, steps * fields, depth, 128), jnp.float32),
            pltpu.VMEM((steps, rows_each, 2 * KC), jnp.float32),
            pltpu.VMEM((steps, rows_each // 2, 2 * KC), jnp.float32),
            pltpu.VMEM((extra, steps, rows_each // 4, 2 * KC), jnp.float32),
            pltpu.VMEM((steps, rows_each // 2, 2 * KC), jnp.float32),
            pltpu.VMEM((bits - 1, steps, rows_each // 4, 2 * KC), jnp.float32),
            pltpu.VMEM((steps, rows_each, 2 * KC), jnp.bfloat16),
            dma((2, steps)),
            dma((2, steps)),
            dma((2, steps)),
            dma((2,)),
            dma((2,)),
            dma((bits, steps)),
            dma((bits, steps)),
            dma((2, steps)),
            dma((2, steps)),
            dma((steps,)),
        ],
        compiler_params=pltpu.CompilerParams(
            collective_id=0, has_side_effects=True, vmem_limit_bytes=38 << 20
        ),
        name="step",
    )(
        state_fields.reshape(fields, levels * rows, columns),
        stencil_weights.reshape(4, levels * rows, columns),
        cosines,
        sines,
        turned_cosines,
        turned_sines,
        bounds,
    )
    return advanced.reshape(state_fields.shape)


def solution(mesh):
    return jax.shard_map(
        on_device,
        mesh=mesh,
        in_specs=(P(None, None, "lat", "lon"), P(None, None, "lat", "lon"), P(), P()),
        out_specs=P(None, None, "lat", "lon"),
        check_vma=False,
    )
```

```python
import math

import jax
import jax.numpy as jnp
from jax import lax
from jax.experimental import pallas as pl
from jax.experimental.pallas import tpu as pltpu
from jax.sharding import PartitionSpec as P

KC = 256


def angle_parts(columns, circle_size, axis):
    waves = lax.broadcasted_iota(
        jnp.int32, (columns.size, KC) if axis == 1 else (KC, columns.size), axis
    )
    product = jnp.expand_dims(columns, axis) * waves % circle_size
    angles = product.astype(jnp.float32) * (2.0 * math.pi / circle_size)
    return jnp.cos(angles), jnp.sin(angles)


MESH = pl.DeviceIdType.MESH


def step_kernel(
    state,
    weights,
    cosines,
    sines,
    turned_cosines,
    turned_sines,
    bounds,
    results,
    waves,
    turned,
    rounded,
    top,
    bottom,
    north,
    south,
    columns_out,
    columns_in,
    sides,
    partial,
    halves,
    quarters,
    half_in,
    quarter_in,
    spectra,
    row_send,
    row_recv,
    side_send,
    side_recv,
    sum_send,
    sum_recv,
    join_send,
    join_recv,
):
    fields, lines, columns = state.shape
    chunks, _, size, _ = top.shape
    depth = lines // chunks
    rows = depth // size
    modes = waves.shape[1] // 2
    half = partial.shape[1] // 2
    quarter = half // 2
    lat_count, lon_count = lax.axis_size("lat"), lax.axis_size("lon")
    lat, lon = lax.axis_index("lat"), lax.axis_index("lon")
    after = lax.rem(lon + 1, lon_count)
    before = lax.rem(lon + lon_count - 1, lon_count)
    across = lax.rem(lon + lon_count // 2, lon_count)
    bits = lon_count.bit_length() - 1
    digit = [lax.rem(lon // (1 << b), 2) for b in range(bits)]
    peer = [lon + (1 << b) - (2 << b) * digit[b] for b in range(bits)]
    own_half = digit[0] * half
    own_quarter = digit[1] * quarter

    def span_of(g, first, count):
        return pl.ds(pl.multiple_of(g * depth + first, count), count)

    def remote(source, target, sent, got, device):
        return pltpu.make_async_remote_copy(
            src_ref=source,
            dst_ref=target,
            send_sem=sent,
            recv_sem=got,
            device_id=device,
            device_id_type=MESH,
        )

    def row_copy(g, up, device, into_north):
        return remote(
            top.at[g] if up else bottom.at[g],
            north.at[g] if into_north else south.at[g],
            row_send.at[0 if up else 1, g],
            row_recv.at[0 if into_north else 1, g],
            device,
        )

    def side_copy(k, device):
        return remote(
            columns_out.at[k], columns_in.at[k], side_send.at[k], side_recv.at[k], device
        )

    def sum_copy(b, g):
        if b == 0:
            away = pl.ds(pl.multiple_of((1 - digit[0]) * half, 16), half)
            source, target = partial.at[g, away], half_in.at[g]
        elif b == 1:
            away = pl.ds(pl.multiple_of((1 - digit[1]) * quarter, 16), quarter)
            source, target = halves.at[g, away], quarter_in.at[0, g]
        else:
            source, target = quarters.at[b - 2, g], quarter_in.at[b - 1, g]
        return remote(source, target, sum_send.at[b, g], sum_recv.at[b, g], (lat, peer[b]))

    def join_copy(b, g):
        if b == 0:
            part = pl.ds(pl.multiple_of(own_half, 16), half)
        else:
            part = pl.ds(pl.multiple_of(own_half + own_quarter, 16), quarter)
        view = spectra.at[g, part]
        return remote(view, view, join_send.at[b, g], join_recv.at[b, g], (lat, peer[b]))

    barrier = pltpu.get_barrier_semaphore()
    for other in (after, before, across, *peer):
        pl.semaphore_signal(barrier, inc=1, device_id=(lat, other), device_id_type=MESH)

    @pl.when(lat > 0)
    def _():
        pl.semaphore_signal(barrier, inc=1, device_id=(lat - 1, lon), device_id_type=MESH)

    @pl.when(lat < lat_count - 1)
    def _():
        pl.semaphore_signal(barrier, inc=1, device_id=(lat + 1, lon), device_id_type=MESH)

    inside = (lat > 0) & (lat < lat_count - 1)

    @pl.when(inside)
    def _():
        pl.semaphore_wait(barrier, 5 + bits)

    @pl.when(jnp.logical_not(inside))
    def _():
        pl.semaphore_wait(barrier, 4 + bits)

    taker = lax.broadcasted_iota(jnp.int32, (2 * size, depth), 0)
    taken = lax.broadcasted_iota(jnp.int32, (2 * size, depth), 1)
    wanted = jnp.where(taker < size, taker * rows, (taker - size) * rows + rows - 1)
    gather = jnp.where(taken == wanted, 1.0, 0.0).astype(jnp.bfloat16)

    def send_rows(g, carry):
        for field in range(fields):
            sign = -1.0 if field < 2 else 1.0
            up_sign = jnp.where(lat == 0, sign, 1.0).astype(jnp.float32)
            down_sign = jnp.where(lat == lat_count - 1, sign, 1.0).astype(jnp.float32)
            edges = jnp.dot(
                gather,
                state[field, span_of(g, 0, depth)].astype(jnp.bfloat16),
                preferred_element_type=jnp.float32,
            )
            top[g, field] = (edges[:size] * up_sign).astype(jnp.bfloat16)
            bottom[g, field] = (edges[size:] * down_sign).astype(jnp.bfloat16)

        @pl.when(lat == 0)
        def _():
            row_copy(g, True, (lat, across), True).start()

        @pl.when(lat > 0)
        def _():
            row_copy(g, True, (lat - 1, lon), False).start()

        @pl.when(lat < lat_count - 1)
        def _():
            row_copy(g, False, (lat + 1, lon), True).start()

        @pl.when(lat == lat_count - 1)
        def _():
            row_copy(g, False, (lat, across), False).start()

        return carry

    lax.fori_loop(0, chunks, send_rows, 0)

    spot = lax.broadcasted_iota(jnp.int32, (16, 128), 1)
    line = lax.broadcasted_iota(jnp.int32, (16, 128), 0)

    def pick(k, lanes, lane):
        chosen = jnp.where((spot == lane) & (line == 0), 1.0, 0.0).astype(jnp.bfloat16)
        for g in range(chunks):
            for field in range(0, fields):
                first = (g * fields + field) * depth
                edge = state[field, span_of(g, 0, depth), lanes].astype(jnp.bfloat16)
                picked = lax.dot_general(
                    chosen, edge, (((1,), (1,)), ((), ())), preferred_element_type=jnp.float32
                )
                columns_out[k, g * fields + field] = picked.astype(jnp.bfloat16)

    pick(0, pl.ds(columns - 128, 128), 127)
    side_copy(0, (lat, after)).start()
    pick(1, pl.ds(0, 128), 0)
    side_copy(1, (lat, before)).start()

    fine = 32
    coarse = columns // fine
    fine_cos, fine_sin = cosines[coarse:], sines[coarse:]

    def fill(at, carry):
        span = pl.ds(pl.multiple_of(at * fine, fine), fine)
        coarse_cos, coarse_sin = cosines[pl.ds(at, 1)], sines[pl.ds(at, 1)]
        waves[span, :modes] = (coarse_cos * fine_cos - coarse_sin * fine_sin).astype(jnp.bfloat16)
        waves[span, modes:] = (coarse_sin * fine_cos + coarse_cos * fine_sin).astype(jnp.bfloat16)
        return carry

    lax.fori_loop(0, coarse, fill, 0)
    lane_cos, lane_sin = turned_cosines[:, :128], turned_sines[:, :128]
    for at in range(columns // 128):
        span = pl.ds(at * 128, 128)
        tile_cos = turned_cosines[:, 128 + at : 129 + at]
        tile_sin = turned_sines[:, 128 + at : 129 + at]
        turned[:modes, span] = (tile_cos * lane_cos - tile_sin * lane_sin).astype(jnp.bfloat16)
        turned[modes:, span] = (tile_sin * lane_cos + tile_cos * lane_sin).astype(jnp.bfloat16)

    spread = jnp.where(line == 0, 1.0, 0.0).astype(jnp.bfloat16)
    for k in range(2):
        side_copy(k, (lat, after)).wait_recv()
        for at in range(chunks * fields):
            sides[k, at] = lax.dot_general(
                columns_in[k, at],
                spread,
                (((0,), (0,)), ((), ())),
                preferred_element_type=jnp.float32,
            )

    lane = lax.broadcasted_iota(jnp.int32, (rows, columns), 1)
    level_line = lax.broadcasted_iota(jnp.int32, (rows, columns), 0)
    copies = columns // 128

    wave = lax.rem(lax.broadcasted_iota(jnp.int32, (rows, 2 * modes), 1), modes)
    circle_size = columns * lon_count
    weight = jnp.where(wave == 0, 1.0 / circle_size, 2.0 / circle_size)
    scale = jnp.where(wave <= bounds[:, 1:2], weight, 0.0).astype(jnp.float32)

    def advance(g):
        row_copy(g, True, (lat, across), True).wait_recv()
        row_copy(g, False, (lat, across), False).wait_recv()

        def one_field(field, inner):
            above = north[g, field].astype(jnp.float32)
            below = south[g, field].astype(jnp.float32)
            for level in range(0, size, 2):
                pair = []
                for at in (level, level + 1):
                    span = pl.ds(at * rows, rows)
                    here = span_of(g, at * rows, rows)
                    x = state[field, here]
                    left = jnp.concatenate([sides[0, g * fields + field, span]] * copies, axis=1)
                    right = jnp.concatenate([sides[1, g * fields + field, span]] * copies, axis=1)
                    w = jnp.where(lane == 0, left, pltpu.roll(x, 1, 1))
                    e = jnp.where(lane == columns - 1, right, pltpu.roll(x, columns - 1, 1))
                    n = jnp.where(level_line == 0, above[at : at + 1], pltpu.roll(x, 1, 0))
                    s = jnp.where(
                        level_line == rows - 1, below[at : at + 1], pltpu.roll(x, rows - 1, 0)
                    )
                    y = (
                        x
                        + weights[0, here] * (e - x)
                        + weights[1, here] * (w - x)
                        + weights[2, here] * (n - x)
                        + weights[3, here] * (s - x)
                    )
                    results[field, here] = y
                    pair.append(y)
                first = pl.multiple_of(field * depth + level * rows, 2 * rows)
                rounded[pl.ds(first, 2 * rows), :] = jnp.concatenate(pair, axis=0).astype(
                    jnp.bfloat16
                )
            return inner

        lax.fori_loop(0, fields, one_field, 0)
        partial[g] = jnp.dot(rounded[...], waves[...], preferred_element_type=jnp.float32)
        sum_copy(0, g).start()

    def pair_sum(g):
        sum_copy(0, g).wait_recv()
        mine = pl.ds(pl.multiple_of(own_half, 16), half)
        halves[g] = partial[g, mine] + half_in[g]
        sum_copy(1, g).start()

    def full_sum(g):
        sum_copy(1, g).wait_recv()
        mine = pl.ds(pl.multiple_of(own_quarter, 16), quarter)
        total = halves[g, mine] + quarter_in[0, g]
        for b in range(2, bits):
            quarters[b - 2, g] = total
            sum_copy(b, g).start()
            sum_copy(b, g).wait_recv()
            total = total + quarter_in[b - 1, g]
        scaled = total.reshape(quarter // rows, rows, 2 * modes) * scale[None]
        part = pl.ds(pl.multiple_of(own_half + own_quarter, 16), quarter)
        spectra[g, part] = scaled.reshape(quarter, 2 * modes).astype(jnp.bfloat16)
        join_copy(1, g).start()

    def join(g):
        join_copy(1, g).wait_recv()
        join_copy(0, g).start()

    def merge(g):
        join_copy(0, g).wait_recv()
        smooth = jnp.dot(spectra[g], turned[...], preferred_element_type=jnp.float32)
        smooth = smooth.astype(jnp.bfloat16).astype(jnp.float32)
        smooth = smooth.reshape(fields, size, rows, columns)
        kept = jnp.broadcast_to(bounds[:, 0:1], (rows, columns)) != 0
        for field in range(fields):
            for at in range(size):
                here = span_of(g, at * rows, rows)
                results[field, here] = jnp.where(kept, smooth[field, at], results[field, here])

    def forward(t, carry):
        advance(t)

        @pl.when(t >= 1)
        def _():
            pair_sum(t - 1)

        return carry

    last = chunks - 1
    lax.fori_loop(0, chunks, forward, 0)
    full_sum(0)
    pair_sum(last)

    def sums(g, carry):
        full_sum(g)
        return carry

    def joins(g, carry):
        join(g)
        return carry

    def merges(g, carry):
        merge(g)

        @pl.when(g + 2 < chunks)
        def _():
            join(g + 2)

        return carry

    lax.fori_loop(1, last, sums, 0)
    lax.fori_loop(0, 2, joins, 0)
    full_sum(last)
    lax.fori_loop(0, chunks, merges, 0)

    def finish(g, carry):
        for b in range(bits):
            sum_copy(b, g).wait_send()
        for b in range(2):
            join_copy(b, g).wait_send()
        row_copy(g, True, (lat, across), True).wait_send()
        row_copy(g, False, (lat, across), False).wait_send()
        return carry

    lax.fori_loop(0, chunks, finish, 0)
    for k in range(2):
        side_copy(k, (lat, after)).wait_send()


def on_device(state_fields, stencil_weights, filter_mask, cutoff_wave):
    fields, levels, rows, columns = state_fields.shape
    lat_count, lon_count = lax.axis_size("lat"), lax.axis_size("lon")
    lat_pos, lon_pos = lax.axis_index("lat"), lax.axis_index("lon")
    circle_size = columns * lon_count
    size = 8
    steps = levels // size
    start = lat_pos * rows
    bounds = lax.dynamic_slice_in_dim(jnp.stack([filter_mask, cutoff_wave], axis=1), start, rows)
    origin = lon_pos * columns
    cosines, sines = angle_parts(
        jnp.concatenate(
            [origin + 32 * jnp.arange(columns // 32), jnp.arange(32)]
        ).astype(jnp.int32),
        circle_size,
        1,
    )
    turned_cosines, turned_sines = angle_parts(
        jnp.concatenate(
            [jnp.arange(128), origin + 128 * jnp.arange(columns // 128)]
        ).astype(jnp.int32),
        circle_size,
        0,
    )
    rows_each = fields * size * rows
    depth = size * rows
    dma = pltpu.SemaphoreType.DMA
    strip = pltpu.VMEM((steps, fields, size, columns), jnp.bfloat16)
    column_strip = pltpu.VMEM((2, steps * fields, 16, depth), jnp.bfloat16)
    extra = max(lon_count.bit_length() - 3, 1)
    in_vmem = pl.BlockSpec(memory_space=pltpu.VMEM)
    bits = lon_count.bit_length() - 1
    advanced = pl.pallas_call(
        step_kernel,
        in_specs=[in_vmem] * 7,
        out_specs=in_vmem,
        out_shape=jax.ShapeDtypeStruct((fields, levels * rows, columns), jnp.float32),
        scratch_shapes=[
            pltpu.VMEM((columns, 2 * KC), jnp.bfloat16),
            pltpu.VMEM((2 * KC, columns), jnp.bfloat16),
            pltpu.VMEM((rows_each, columns), jnp.bfloat16),
            strip,
            strip,
            strip,
            strip,
            column_strip,
            column_strip,
            pltpu.VMEM((2, steps * fields, depth, 128), jnp.float32),
            pltpu.VMEM((steps, rows_each, 2 * KC), jnp.float32),
            pltpu.VMEM((steps, rows_each // 2, 2 * KC), jnp.float32),
            pltpu.VMEM((extra, steps, rows_each // 4, 2 * KC), jnp.float32),
            pltpu.VMEM((steps, rows_each // 2, 2 * KC), jnp.float32),
            pltpu.VMEM((bits - 1, steps, rows_each // 4, 2 * KC), jnp.float32),
            pltpu.VMEM((steps, rows_each, 2 * KC), jnp.bfloat16),
            dma((2, steps)),
            dma((2, steps)),
            dma((2,)),
            dma((2,)),
            dma((bits, steps)),
            dma((bits, steps)),
            dma((2, steps)),
            dma((2, steps)),
        ],
        compiler_params=pltpu.CompilerParams(
            collective_id=0, has_side_effects=True, vmem_limit_bytes=38 << 20
        ),
        name="step",
    )(
        state_fields.reshape(fields, levels * rows, columns),
        stencil_weights.reshape(4, levels * rows, columns),
        cosines,
        sines,
        turned_cosines,
        turned_sines,
        bounds,
    )
    return advanced.reshape(state_fields.shape)


def solution(mesh):
    return jax.shard_map(
        on_device,
        mesh=mesh,
        in_specs=(P(None, None, "lat", "lon"), P(None, None, "lat", "lon"), P(), P()),
        out_specs=P(None, None, "lat", "lon"),
        check_vma=False,
    )
```
